128 devices in a mesh: group: 8 (over x, z_hi), space: 16 (over y, z_lo, core).
Axes of the slice: x: 4, y: 4, z: 4 (z_hi: 2, z_lo: 2; z = z_hi * 2 + z_lo), core: 2. Of those that a mesh axis runs over, the one named last changes fastest.
Arguments:
- prev_field: float32 [8, 256, 256, 256], P('group', 'space'), may hold values from -6 to 6
- curr_field: float32 [8, 256, 256, 256], P('group', 'space'), may hold values from -6 to 6
- coefficient: float32 [256, 256, 256], P('space'), may hold values from 0.05 to 0.2
- recordings: float32 [8, 2, 512], P('group'), may hold values from -24 to 24
- receivers: int32 [8, 512], P('group'), may hold values from 0 to 16777215
- image_in: float32 [128, 128, 128], P('space', 'group'), may hold values from -6 to 6
Outputs:
- final_field: float32 [8, 256, 256, 256], P('group', 'space')
- image_out: float32 [128, 128, 128], P('space', 'group')
The draws below stay inside these ranges and needn't reach their ends.
All inputs are finite; a program needn't handle non-finite values.
Results may differ from the reference program's by a relative error of at most 0.00002.
Values sent between devices are 32-bit elements; how exact they have to be, the bound alone decides.
A program may use at most 128 MiB of HBM per device.

```python
import jax
import jax.numpy as jnp
from jax import lax

NX = 256
NY = 256
RECV = 512
STEPS = 2
DEC = 2
GROUPS = 8
NZ = 256


def plant(drawn, rng, least, high):
    longest = drawn.shape.index(max(drawn.shape))
    spots = []
    for shift in (0, 1):
        where = [jax.random.randint(jax.random.fold_in(rng, axis), (), 0, length) for axis, length in enumerate(drawn.shape)]
        where[longest] = (where[longest] + shift) % drawn.shape[longest]
        spots.append(tuple(where))
    return drawn.at[spots[0]].set(least).at[spots[1]].set(high)


def steps_of(key, dims, shards, smallest, high):
    def one(dim, shards_of):
        steps = jax.random.uniform(jax.random.fold_in(jax.random.fold_in(key, 6), dim), (shards_of,), jnp.float32, smallest / len(shards), high / len(shards))
        return jnp.repeat(jnp.exp(steps), dims[dim] // shards_of).reshape((-1,) + (1,) * (len(dims) - dim - 1))

    loudness = one(*shards[0])
    for cut in shards[1:]:
        loudness = loudness * one(*cut)
    return loudness


def scatter_about(stream_key, dims, width, reach, split=(), kind=jnp.bfloat16):
    result = jax.random.normal(stream_key, dims, jnp.float32) * width
    if len(split) > 0:
        result = steps_of(stream_key, dims, split, -0.22, 0.18) * result
    return jnp.clip(result, min=-reach, max=reach).astype(kind)


def setup_inputs(seed: int = 0) -> dict:
    key_list = jax.random.split(jax.random.key(seed), 7)
    return {
        "prev_field": scatter_about(key_list[0], (GROUPS, NZ, NX, NY), 1.0, 6.0, ((0, 8), (1, 16)), jnp.float32),
        "curr_field": scatter_about(key_list[1], (GROUPS, NZ, NX, NY), 1.0, 6.0, ((0, 8), (1, 16)), jnp.float32),
        "coefficient": jnp.clip(0.05 + 0.15 * jax.random.uniform(key_list[2], (NZ, NX, NY), jnp.float32) ** steps_of(key_list[2], (NZ, NX, NY), ((0, 16),), -0.2, 0.2), 0.05, 0.2),
        "recordings": scatter_about(key_list[3], (GROUPS, STEPS, RECV), 4.0, 24.0, ((0, 8),), jnp.float32),
        "receivers": plant(jax.random.randint(key_list[4], (GROUPS, RECV), 0, NZ * NX * NY), jax.random.fold_in(key_list[4], 1), 0, (NZ * NX * NY) - 1).astype(jnp.int32),
        "image_in": scatter_about(key_list[5], (NZ // DEC, NX // DEC, NY // DEC), 1.0, 6.0, ((0, 16), (1, 8)), jnp.float32),
    }


COEF = (-205.0 / 72.0, 8.0 / 5.0, -1.0 / 5.0, 8.0 / 315.0, -1.0 / 560.0)


def laplace(zpadded):
    nz = zpadded.shape[0] - 8
    nx = zpadded.shape[1]
    ny = zpadded.shape[2]
    full = jnp.pad(zpadded, ((0, 0), (4, 4), (4, 4)))
    centre = zpadded[4:4 + nz]
    total = (3.0 * COEF[0]) * centre
    for j in range(1, 5):
        side = zpadded[4 + j:4 + j + nz] + zpadded[4 - j:4 - j + nz]
        side = side + full[4:4 + nz, 4 + j:4 + j + nx, 4:4 + ny] + full[4:4 + nz, 4 - j:4 - j + nx, 4:4 + ny]
        side = side + full[4:4 + nz, 4:4 + nx, 4 + j:4 + j + ny] + full[4:4 + nz, 4:4 + nx, 4 - j:4 - j + ny]
        total = total + COEF[j] * side
    return total


def reference(prev_field, curr_field, coefficient, recordings, receivers, image_in):
    coef_flat = coefficient.reshape(-1)

    def run_group(items):
        prev, curr, record, index = items
        for step in range(STEPS):
            padded = jnp.pad(curr, ((4, 4), (0, 0), (0, 0)))
            nxt = 2.0 * curr - prev + coefficient * laplace(padded)
            amount = coef_flat[index] * record[step]
            nxt = nxt.reshape(-1).at[index].add(amount).reshape(curr.shape)
            prev, curr = curr, nxt
        sample = curr[::DEC, ::DEC, ::DEC]
        return curr, jnp.log(1.0 + sample * sample)

    final_field, terms = lax.map(run_group, (prev_field, curr_field, recordings, receivers))
    image_out = image_in + (jnp.exp(jnp.mean(terms, axis=0)) - 1.0)
    return final_field, image_out
```

```python
import functools

import jax
import jax.numpy as jnp
from jax import lax
from jax.experimental import pallas as pl
from jax.experimental.pallas import tpu as pltpu
from jax.sharding import PartitionSpec as P

SCALE = 5040.0
TAPS = (8064.0, -1008.0, 128.0, -9.0)
CENTRE = 3.0 * -14350.0
PAD = 4
CHUNKS = 8
NT = (((1,), (1,)), ((), ()))


def dot(a, b):
    return jnp.dot(a, b, preferred_element_type=jnp.float32)


def dot_nt(a, b):
    return lax.dot_general(a, b, NT, preferred_element_type=jnp.float32)


def split2(v):
    high = v.astype(jnp.bfloat16)
    return high, (v - high.astype(jnp.float32)).astype(jnp.bfloat16)


def kernel(
    prev_hbm, curr_hbm, coef_hbm, rec_ref, idx_ref, image_ref,
    field_hbm, image_out,
    older, newer, coef, halo, mixed, band, amounts, terms, from_x, from_z,
    load_sem, store_sem, halo_send, halo_recv, x_send, x_recv, z_send, z_recv,
):
    depth, nx, ny = coef.shape
    rows = nx // CHUNKS
    slabs = lax.axis_size("space")
    group = lax.axis_index("group")
    slab = lax.axis_index("space")
    my_x, my_z = group // 2, lax.rem(group, 2)
    has_low, has_high = slab > 0, slab < slabs - 1

    loads = [
        pltpu.make_async_copy(curr_hbm.at[0], newer.at[pl.ds(PAD, depth)], load_sem.at[0]),
        pltpu.make_async_copy(coef_hbm, coef, load_sem.at[1]),
        pltpu.make_async_copy(prev_hbm.at[0], older.at[pl.ds(PAD, depth)], load_sem.at[2]),
    ]
    for load in loads:
        load.start()

    barrier = pltpu.get_barrier_semaphore()

    @pl.when(has_low)
    def _():
        pl.semaphore_signal(barrier, inc=1, device_id={"space": slab - 1})

    @pl.when(has_high)
    def _():
        pl.semaphore_signal(barrier, inc=1, device_id={"space": slab + 1})

    for hop in range(1, 4):
        pl.semaphore_signal(barrier, inc=1, device_id={"group": lax.rem(my_x + hop, 4) * 2 + my_z})
    pl.semaphore_signal(barrier, inc=1, device_id={"group": my_x * 2 + 1 - my_z})
    pl.semaphore_wait(barrier, 4 + has_low.astype(jnp.int32) + has_high.astype(jnp.int32))

    def chunk_of(i):
        return lax.rem(my_x + 1 + i // 2, 4) * 2 + lax.rem(my_z + 1 + i, 2)

    def rows_of(i):
        return pl.ds(pl.multiple_of(chunk_of(i) * rows, rows), rows)

    def to_low(step, i):
        source = curr_hbm.at[0, pl.ds(0, PAD), rows_of(i)] if step == 0 else older.at[pl.ds(PAD, PAD), rows_of(i)]
        return pltpu.make_async_remote_copy(
            source, halo.at[step, 1, :, rows_of(i)], halo_send.at[step, 0, i], halo_recv.at[step, 1, i],
            device_id={"space": slab - 1},
        )

    def to_high(step, i):
        source = (
            curr_hbm.at[0, pl.ds(depth - PAD, PAD), rows_of(i)] if step == 0 else older.at[pl.ds(depth, PAD), rows_of(i)]
        )
        return pltpu.make_async_remote_copy(
            source, halo.at[step, 0, :, rows_of(i)], halo_send.at[step, 1, i], halo_recv.at[step, 0, i],
            device_id={"space": slab + 1},
        )

    def send(step, i):
        @pl.when(has_low)
        def _():
            to_low(step, i).start()

        @pl.when(has_high)
        def _():
            to_high(step, i).start()

    @pl.loop(0, CHUNKS)
    def _(i):
        send(0, i)

    for ref in (older, newer):
        zero = jnp.zeros((PAD, nx, ny), jnp.float32)
        ref[pl.ds(0, PAD)] = zero
        ref[pl.ds(PAD + depth, PAD)] = zero
    apart = jnp.abs(
        lax.broadcasted_iota(jnp.int32, (nx, nx), 0) - lax.broadcasted_iota(jnp.int32, (nx, nx), 1)
    )
    matrix = jnp.zeros((nx, nx), jnp.float32)
    for j, tap in enumerate(TAPS):
        matrix = jnp.where(apart == j + 1, tap, matrix)
    band[...] = matrix.astype(jnp.bfloat16)
    index = idx_ref[...]
    receivers = index.shape[1]
    at_y = lax.broadcasted_iota(jnp.int32, (ny, receivers), 0) == (index & (ny - 1))
    for step in range(2):
        high, low = split2(rec_ref[0, pl.ds(step, 1), :] * SCALE)
        amounts[step, 0] = jnp.where(at_y, high.astype(jnp.float32), 0.0).astype(jnp.bfloat16)
        amounts[step, 1] = jnp.where(at_y, low.astype(jnp.float32), 0.0).astype(jnp.bfloat16)

    for load in loads:
        load.wait()

    def base(step, field, other):
        @pl.loop(0, depth)
        def _(z):
            high, low = split2(field[z + PAD])
            first = (slab * depth + z) * nx
            at_row = lax.broadcasted_iota(jnp.int32, (nx, receivers), 0) + first == (index >> 8)
            onehot = jnp.where(at_row, 1.0, 0.0).astype(jnp.bfloat16)
            mixed[...] = (
                dot(high, band[...]) + dot(low, band[...])
                + dot(band[...], high) + dot(band[...], low)
                + dot_nt(onehot, amounts[step, 0]) + dot_nt(onehot, amounts[step, 1])
            )

            @pl.loop(0, CHUNKS)
            def _(b):
                part = pl.ds(pl.multiple_of(b * rows, rows), rows)
                centre = field[z + PAD, part]
                total = CENTRE * centre + mixed[part]
                for j, tap in enumerate(TAPS):
                    total += tap * (field[z + PAD + j + 1, part] + field[z + PAD - j - 1, part])
                other[z + PAD, part] = 2.0 * centre - other[z + PAD, part] + (coef[z, part] * (1.0 / SCALE)) * total

    def add_halo(step, i, other):
        part = rows_of(i)

        @pl.when(has_low)
        def _():
            to_high(step, i).wait_recv()
            for k in range(PAD):
                total = TAPS[k] * halo[step, 0, PAD - 1, part]
                for j in range(k + 1, PAD):
                    total += TAPS[j] * halo[step, 0, PAD + k - j - 1, part]
                other[PAD + k, part] += (coef[k, part] * (1.0 / SCALE)) * total

        @pl.when(has_high)
        def _():
            to_low(step, i).wait_recv()
            for k in range(PAD):
                total = TAPS[k] * halo[step, 1, 0, part]
                for j in range(k + 1, PAD):
                    total += TAPS[j] * halo[step, 1, j - k, part]
                z = depth - 1 - k
                other[PAD + z, part] += (coef[z, part] * (1.0 / SCALE)) * total

    base(0, newer, older)

    @pl.loop(0, CHUNKS)
    def _(i):
        add_halo(0, i, older)
        send(1, i)

    base(1, older, newer)

    half = rows // 2
    planes = depth // 2
    even = jnp.where(
        lax.broadcasted_iota(jnp.int32, (ny // 2, ny), 1) == 2 * lax.broadcasted_iota(jnp.int32, (ny // 2, ny), 0), 1.0, 0.0
    ).astype(jnp.bfloat16)

    def store(i):
        return pltpu.make_async_copy(
            newer.at[pl.ds(PAD, depth), rows_of(i)], field_hbm.at[0, :, rows_of(i)], store_sem.at[i]
        )

    def term_of(i):
        add_halo(1, i, newer)
        store(i).start()
        part = rows_of(i)
        rest = jnp.concatenate([newer[PAD + 2 * p, part] for p in range(planes)], axis=0)
        sample = None
        for _ in range(3):
            piece = rest.astype(jnp.bfloat16)
            rest = rest - piece.astype(jnp.float32)
            picked = dot(even, dot_nt(piece, even).astype(jnp.bfloat16))
            sample = picked if sample is None else sample + picked
        return jnp.log(1.0 + sample * sample).reshape(planes, half, ny // 2)

    def to_x(i):
        other_x = chunk_of(i) // 2
        other_z = lax.rem(chunk_of(i), 2)
        return pltpu.make_async_remote_copy(
            terms.at[i], from_x.at[other_z, my_x], x_send.at[i], x_recv.at[other_z, my_x],
            device_id={"group": other_x * 2 + my_z},
        )

    @pl.loop(0, CHUNKS - 2)
    def _(i):
        terms[i] = term_of(i)
        to_x(i).start()

    def sum_x(total, which):
        for hop in range(1, 4):
            other_x = lax.rem(my_x + hop, 4)
            pltpu.make_async_remote_copy(
                terms.at[0], from_x.at[which, other_x], x_send.at[0], x_recv.at[which, other_x],
                device_id={"group": other_x * 2 + my_z},
            ).wait_recv()
            total += from_x[which, other_x]
        return total

    to_z = pltpu.make_async_remote_copy(
        terms.at[CHUNKS - 2], from_z, z_send, z_recv, device_id={"group": my_x * 2 + 1 - my_z}
    )
    terms[CHUNKS - 2] = sum_x(term_of(CHUNKS - 2), 1 - my_z)
    to_z.start()
    total = sum_x(term_of(CHUNKS - 1), my_z)
    to_z.wait_recv()
    total += from_z[...]
    image_out[...] = image_ref[...] + (jnp.exp(total * 0.125) - 1.0)

    to_z.wait_send()

    @pl.loop(0, CHUNKS - 2)
    def _(i):
        to_x(i).wait_send()

    @pl.loop(0, CHUNKS)
    def _(i):
        store(i).wait()
        for step in range(2):
            @pl.when(has_low)
            def _():
                to_low(step, i).wait_send()

            @pl.when(has_high)
            def _():
                to_high(step, i).wait_send()


def on_device(prev_field, curr_field, coefficient, recordings, receivers, image_in):
    depth, nx, ny = coefficient.shape
    _, steps, count = recordings.shape
    padded = (depth + 2 * PAD, nx, ny)
    image = image_in.shape
    anywhere = pl.BlockSpec(memory_space=pl.ANY)
    vmem = pl.BlockSpec(memory_space=pltpu.VMEM)
    dma = pltpu.SemaphoreType.DMA
    return pl.pallas_call(
        kernel,
        out_shape=(
            jax.ShapeDtypeStruct(curr_field.shape, jnp.float32),
            jax.ShapeDtypeStruct(image, jnp.float32),
        ),
        in_specs=[anywhere, anywhere, anywhere, vmem, vmem, vmem],
        out_specs=(anywhere, vmem),
        scratch_shapes=[
            pltpu.VMEM(padded, jnp.float32),
            pltpu.VMEM(padded, jnp.float32),
            pltpu.VMEM((depth, nx, ny), jnp.float32),
            pltpu.VMEM((steps, 2, PAD, nx, ny), jnp.float32),
            pltpu.VMEM((nx, ny), jnp.float32),
            pltpu.VMEM((nx, nx), jnp.bfloat16),
            pltpu.VMEM((steps, 2, ny, count), jnp.bfloat16),
            pltpu.VMEM((CHUNKS,) + image, jnp.float32),
            pltpu.VMEM((2, 4) + image, jnp.float32),
            pltpu.VMEM(image, jnp.float32),
            dma((3,)), dma((CHUNKS,)),
            dma((steps, 2, CHUNKS)), dma((steps, 2, CHUNKS)),
            dma((CHUNKS,)), dma((2, 4)), dma, dma,
        ],
        compiler_params=pltpu.CompilerParams(
            collective_id=0, has_side_effects=True, vmem_limit_bytes=56 * 1024 * 1024
        ),
    )(prev_field, curr_field, coefficient, recordings, receivers, image_in)


def solution(mesh):
    placed = (
        P("group", "space", None, None),
        P("group", "space", None, None),
        P("space", None, None),
        P("group", None, None),
        P("group", None),
        P("space", "group", None),
    )
    return jax.shard_map(
        on_device,
        mesh=mesh,
        in_specs=placed,
        out_specs=(P("group", "space", None, None), P("space", "group", None)),
        check_vma=False,
    )
```

```python
import jax
import jax.numpy as jnp
from jax import lax
from jax.experimental import pallas as pl
from jax.experimental.pallas import tpu as pltpu
from jax.sharding import PartitionSpec as P

SCALE = 5040.0
TAPS = (8064.0, -1008.0, 128.0, -9.0)
CENTRE = 3.0 * -14350.0
PAD = 4
CHUNKS = 8
ROWS = 4
BLOCK = 32
NT = (((1,), (1,)), ((), ()))


def dot(a, b):
    return jnp.dot(a, b, preferred_element_type=jnp.float32)


def dot_nt(a, b):
    return lax.dot_general(a, b, NT, preferred_element_type=jnp.float32)


def split2(v):
    high = v.astype(jnp.bfloat16)
    return high, (v - high.astype(jnp.float32)).astype(jnp.bfloat16)


def iota(shape, dim):
    return lax.broadcasted_iota(jnp.int32, shape, dim)


def kernel(
    prev_hbm, curr_hbm, coef_hbm, rec_ref, idx_ref, image_ref,
    field, image_out,
    older, newer, coef, far, near, relay, mixed, band, amounts, early, late, from_x, from_z, from_late,
    load_sem, far_send, far_recv, near_send, near_recv, via_recv, pass_send,
    x_send, x_recv, z_send, z_recv, late_send, late_recv,
):
    depth, nx, ny = coef.shape
    rows = nx // CHUNKS
    slabs = lax.axis_size("space")
    group = lax.axis_index("group")
    slab = lax.axis_index("space")
    my_x, my_z = group // 2, lax.rem(group, 2)
    core = lax.rem(slab, 2)
    far_slab, near_slab = slab - 1 + 2 * core, slab + 1 - 2 * core
    has_far = (slab > 0) & (slab < slabs - 1)
    far_start, near_start = core * (depth - PAD), (1 - core) * (depth - PAD)

    row, place = slab // 4, lax.rem(slab, 4)
    corner = (place == 0) | (place == 3)
    turn = 1 - 2 * core
    by_relay = jnp.where(corner, core * (2 * ROWS - 2 - 2 * row) + (1 - core) * 2 * row, 0)
    relayed = jnp.where(corner, (1 - core) * (2 * ROWS - 2 - 2 * row) + core * 2 * row, 0)
    partner, onward, behind = slab + 3 * turn, slab + 4 * turn, slab - 4 * turn
    has_onward = corner & (onward >= 0) & (onward < slabs)
    has_behind = corner & (behind >= 0) & (behind < slabs)

    def plane(p):
        return p + core * (depth - 1 - 2 * p)

    loads = [
        pltpu.make_async_copy(curr_hbm.at[0], newer.at[pl.ds(PAD, depth)], load_sem.at[0]),
        pltpu.make_async_copy(coef_hbm, coef, load_sem.at[1]),
        pltpu.make_async_copy(prev_hbm.at[0], older.at[pl.ds(PAD, depth)], load_sem.at[2]),
    ]
    for load in loads:
        load.start()

    barrier = pltpu.get_barrier_semaphore()

    def greet(there, slab_id):
        @pl.when(there)
        def _():
            pl.semaphore_signal(barrier, inc=1, device_id={"space": slab_id})

    pl.semaphore_signal(barrier, inc=1, device_id={"space": near_slab})
    greet(has_far, far_slab)
    greet(corner, partner)
    greet(has_onward, onward)
    greet(has_behind, behind)
    for hop in range(1, 8):
        pl.semaphore_signal(barrier, inc=1, device_id={"group": lax.rem(group + hop, 8)})
    pl.semaphore_wait(barrier, 8 + sum(there.astype(jnp.int32) for there in (has_far, corner, has_onward, has_behind)))

    def chunk_of(i):
        return lax.rem(my_x + 1 + i, 4) * 2 + lax.rem(my_z + 1 + i // 4, 2)

    def rows_of(i):
        return pl.ds(pl.multiple_of(chunk_of(i) * rows, rows), rows)

    def face(step, i):
        if step == 0:
            return curr_hbm.at[0, pl.ds(far_start, PAD), rows_of(i)]
        return older.at[pl.ds(PAD + far_start, PAD), rows_of(i)]

    def far_copy(step, i):
        return pltpu.make_async_remote_copy(
            face(step, i), far.at[step, :, rows_of(i)], far_send.at[step, i], far_recv.at[step, i],
            device_id={"space": far_slab},
        )

    def via_copy(step, i):
        return pltpu.make_async_remote_copy(
            face(step, i), relay.at[step, :, rows_of(i)], far_send.at[step, i], via_recv.at[step, i],
            device_id={"space": partner},
        )

    def pass_copy(step, i):
        return pltpu.make_async_remote_copy(
            relay.at[step, :, rows_of(i)], far.at[step, :, rows_of(i)], pass_send.at[step, i], far_recv.at[step, i],
            device_id={"space": onward},
        )

    def send_far(step, i):
        @pl.when(i < by_relay)
        def _():
            via_copy(step, i).start()

        @pl.when(i >= by_relay)
        def _():
            far_copy(step, i).start()

    def pass_on(step):
        @pl.loop(0, relayed)
        def _(i):
            via_copy(step, i).wait_recv()
            pass_copy(step, i).start()

    def near_copy(step):
        source = curr_hbm.at[0, pl.ds(near_start, PAD)] if step == 0 else older.at[pl.ds(PAD + near_start, PAD)]
        return pltpu.make_async_remote_copy(
            source, near.at[step], near_send.at[step], near_recv.at[step], device_id={"space": near_slab}
        )

    @pl.when(has_far)
    def _():
        @pl.loop(0, CHUNKS)
        def _(i):
            send_far(0, i)

    near_copy(0).start()

    for ref in (older, newer):
        zero = jnp.zeros((PAD, nx, ny), jnp.float32)
        ref[pl.ds(0, PAD)] = zero
        ref[pl.ds(PAD + depth, PAD)] = zero
    apart = jnp.abs(iota((nx, nx), 0) - iota((nx, nx), 1))
    matrix = jnp.zeros((nx, nx), jnp.float32)
    for j, tap in enumerate(TAPS):
        matrix = jnp.where(apart == j + 1, tap, matrix)
    band[...] = matrix.astype(jnp.bfloat16)
    index = idx_ref[...]
    receivers = index.shape[1]
    at_y = iota((ny, receivers), 0) == (index & (ny - 1))
    for step in range(2):
        high, low = split2(rec_ref[0, pl.ds(step, 1), :] * SCALE)
        amounts[step, 0] = jnp.where(at_y, high.astype(jnp.float32), 0.0).astype(jnp.bfloat16)
        amounts[step, 1] = jnp.where(at_y, low.astype(jnp.float32), 0.0).astype(jnp.bfloat16)

    for load in loads:
        load.wait()

    def mix(step, field_ref, z):
        value = field_ref[pl.ds(z + PAD, PAD)].reshape(PAD * nx, ny)
        high, low = split2(value)
        along_y = dot(high, band[...]) + dot(low, band[...])
        beside = [jnp.concatenate([v[k * nx : (k + 1) * nx] for k in range(PAD)], axis=1) for v in (high, low)]
        along_x = dot(band[...], beside[0]) + dot(band[...], beside[1])
        at_row = iota((PAD * nx, receivers), 0) + (slab * depth + z) * nx == (index >> 8)
        onehot = jnp.where(at_row, 1.0, 0.0).astype(jnp.bfloat16)
        injected = dot_nt(onehot, amounts[step, 0]) + dot_nt(onehot, amounts[step, 1])
        for k in range(PAD):
            mixed[z + k] = (along_y + injected)[k * nx : (k + 1) * nx] + along_x[:, k * ny : (k + 1) * ny]

    def update(z, field_ref, old_ref, old_pad, new_ref, new_pad):
        @pl.loop(0, nx // BLOCK)
        def _(b):
            part = pl.ds(pl.multiple_of(b * BLOCK, BLOCK), BLOCK)
            window = [field_ref[z + k, part] for k in range(3 * PAD)]
            for k in range(PAD):
                centre = window[k + PAD]
                total = CENTRE * centre + mixed[z + k, part]
                for j, tap in enumerate(TAPS):
                    total += tap * (window[k + PAD + j + 1] + window[k + PAD - j - 1])
                new_ref[z + k + new_pad, part] = (
                    2.0 * centre - old_ref[z + k + old_pad, part] + (coef[z + k, part] * (1.0 / SCALE)) * total
                )

    quads = depth // PAD

    def quad(g):
        return pl.multiple_of((g + core * (quads - 1 - 2 * g)) * PAD, PAD)

    @pl.loop(0, quads)
    def _(g):
        mix(0, newer, g * PAD)
        update(g * PAD, newer, older, PAD, older, PAD)

    def add_halo(h, z_of, target, pad, part):
        for k in range(PAD):
            total = TAPS[k] * h(0, part)
            for j in range(k + 1, PAD):
                total += TAPS[j] * h(j - k, part)
            z = z_of(k)
            target[z + pad, part] += (coef[z, part] * (1.0 / SCALE)) * total

    def add_near(step, target, pad):
        near_copy(step).wait_recv()

        @pl.loop(0, nx // BLOCK)
        def _(b):
            add_halo(
                lambda k, part: near[step, k + core * (PAD - 1 - 2 * k), part],
                lambda k: plane(depth - 1 - k),
                target, pad, pl.ds(pl.multiple_of(b * BLOCK, BLOCK), BLOCK),
            )

    def add_far(step, i, target, pad):
        far_copy(step, i).wait_recv()
        add_halo(
            lambda k, part: far[step, (PAD - 1 - k) + core * (2 * k - PAD + 1), part],
            plane, target, pad, rows_of(i),
        )

    add_near(0, older, PAD)
    near_copy(1).start()
    pass_on(0)

    @pl.loop(1, quads)
    def _(g):
        mix(1, older, quad(g))

    @pl.loop(2, quads)
    def _(g):
        update(quad(g), older, newer, PAD, field.at[0], 0)

    @pl.when(has_far)
    def _():
        @pl.loop(0, CHUNKS)
        def _(i):
            add_far(0, i, older, PAD)
            send_far(1, i)

    mix(1, older, quad(0))

    @pl.loop(0, 2)
    def _(g):
        update(quad(g), older, newer, PAD, field.at[0], 0)

    add_near(1, field.at[0], 0)

    half = rows // 2
    even = jnp.where(iota((ny // 2, ny), 1) == 2 * iota((ny // 2, ny), 0), 1.0, 0.0).astype(jnp.bfloat16)

    def terms_of(planes):
        size = planes[0].shape[0]
        value = jnp.concatenate(planes, axis=0)
        pieces = []
        for _ in range(3):
            pieces.append(value.astype(jnp.bfloat16))
            value = value - pieces[-1].astype(jnp.float32)
        columns = dot_nt(jnp.concatenate(pieces, axis=0), even).astype(jnp.bfloat16)
        count = 3 * len(planes)
        columns = jnp.concatenate([columns[n * size : (n + 1) * size] for n in range(count)], axis=1)
        picked = dot(even[: size // 2, :size], columns)
        width = ny // 2
        result = []
        for k in range(len(planes)):
            one, two, three = (picked[:, (k + p * len(planes)) * width :][:, :width] for p in range(3))
            sample = one + two + three
            result.append(jnp.log(1.0 + sample * sample))
        return result

    count = PAD // 2
    first_early, first_late = (1 - core) * count, core * (depth // 2 - count)

    @pl.loop(0, depth // 2 - count, step=2)
    def _(q):
        for k, term in enumerate(terms_of([field[0, 2 * (first_early + q + k)] for k in range(2)])):
            early[:, q + k] = term.reshape(CHUNKS, half, ny // 2)

    def to_x(hop, which):
        other = lax.rem(my_x + hop, 4)
        return pltpu.make_async_remote_copy(
            early.at[other * 2 + which], from_x.at[which, hop - 1], x_send.at[which, hop - 1], x_recv.at[which, hop - 1],
            device_id={"group": other * 2 + my_z},
        )

    away, mine = my_x * 2 + 1 - my_z, group
    to_z = pltpu.make_async_remote_copy(early.at[away], from_z, z_send, z_recv, device_id={"group": away})

    @pl.loop(0, 6)
    def _(n):
        to_x(1 + n // 2, lax.rem(n, 2)).start()

    def sum_x(which):
        total = early[my_x * 2 + which]
        for hop in range(1, 4):
            to_x(hop, which).wait_recv()
            total += from_x[which, hop - 1]
        return total

    def late_terms(i):
        @pl.when(has_far)
        def _():
            add_far(1, i, field.at[0], 0)

        part = rows_of(i)
        return terms_of([field[0, 2 * (first_late + q), part] for q in range(count)])

    def to_owner(i):
        return pltpu.make_async_remote_copy(
            late.at[i], from_late.at[i], late_send.at[i], late_recv.at[i], device_id={"group": chunk_of(i)}
        )

    def late_chunk(i):
        for q, term in enumerate(late_terms(i)):
            late[i, q] = term
        to_owner(i).start()

    pass_on(1)

    @pl.loop(0, 4)
    def _(i):
        late_chunk(i)

    early[away] = sum_x(1 - my_z)
    to_z.start()
    early[mine] = sum_x(my_z)

    @pl.loop(4, CHUNKS - 1)
    def _(i):
        late_chunk(i)

    to_z.wait_recv()
    at_early = pl.ds(first_early, depth // 2 - count)
    image_out[at_early] = image_ref[at_early] + (jnp.exp((early[mine] + from_z[...]) * 0.125) - 1.0)
    last = late_terms(CHUNKS - 1)
    for i in range(CHUNKS - 1):
        to_owner(i).wait_recv()
    for q in range(count):
        total = last[q]
        for i in range(CHUNKS - 1):
            total += from_late[i, q]
        image_out[first_late + q] = image_ref[first_late + q] + (jnp.exp(total * 0.125) - 1.0)

    to_z.wait_send()
    for step in range(2):
        near_copy(step).wait_send()

    @pl.loop(0, 6)
    def _(n):
        to_x(1 + n // 2, lax.rem(n, 2)).wait_send()

    @pl.loop(0, CHUNKS - 1)
    def _(i):
        to_owner(i).wait_send()

    for step in range(2):
        @pl.loop(0, relayed)
        def _(i):
            pass_copy(step, i).wait_send()

    @pl.when(has_far)
    def _():
        @pl.loop(0, CHUNKS)
        def _(i):
            for step in range(2):
                far_copy(step, i).wait_send()


def write_out(field, image, field_hbm, image_hbm, sems):
    parts = sems.shape[0] - 1
    planes = field.shape[1] // parts
    copies = [
        pltpu.make_async_copy(field.at[:, pl.ds(i * planes, planes)], field_hbm.at[:, pl.ds(i * planes, planes)], sems.at[i])
        for i in range(parts)
    ]
    copies.append(pltpu.make_async_copy(image, image_hbm, sems.at[parts]))
    for copy in copies:
        copy.start()
    for copy in copies:
        copy.wait()


def on_device(prev_field, curr_field, coefficient, recordings, receivers, image_in):
    depth, nx, ny = coefficient.shape
    _, steps, count = recordings.shape
    padded = (depth + 2 * PAD, nx, ny)
    image = image_in.shape
    early, late = (image[0] - PAD // 2,) + image[1:], (PAD // 2,) + image[1:]
    anywhere = pl.BlockSpec(memory_space=pl.ANY)
    vmem = pl.BlockSpec(memory_space=pltpu.VMEM)
    dma = pltpu.SemaphoreType.DMA
    f32 = jnp.float32
    field, image_out = pl.pallas_call(
        kernel,
        out_shape=(pltpu.VMEM(curr_field.shape, f32), pltpu.VMEM(image, f32)),
        in_specs=[anywhere, anywhere, anywhere, vmem, vmem, vmem],
        out_specs=(vmem, vmem),
        scratch_shapes=[
            pltpu.VMEM(padded, f32),
            pltpu.VMEM(padded, f32),
            pltpu.VMEM((depth, nx, ny), f32),
            pltpu.VMEM((steps, PAD, nx, ny), f32),
            pltpu.VMEM((steps, PAD, nx, ny), f32),
            pltpu.VMEM((steps, PAD, nx, ny), f32),
            pltpu.VMEM((depth, nx, ny), f32),
            pltpu.VMEM((nx, nx), jnp.bfloat16),
            pltpu.VMEM((steps, 2, ny, count), jnp.bfloat16),
            pltpu.VMEM((CHUNKS,) + early, f32),
            pltpu.VMEM((CHUNKS - 1,) + late, f32),
            pltpu.VMEM((2, 3) + early, f32),
            pltpu.VMEM(early, f32),
            pltpu.VMEM((CHUNKS - 1,) + late, f32),
            dma((3,)), dma((steps, CHUNKS)), dma((steps, CHUNKS)), dma((steps,)), dma((steps,)),
            dma((steps, CHUNKS)), dma((steps, CHUNKS)),
            dma((2, 3)), dma((2, 3)), dma, dma, dma((CHUNKS - 1,)), dma((CHUNKS - 1,)),
        ],
        compiler_params=pltpu.CompilerParams(
            collective_id=0, has_side_effects=True, vmem_limit_bytes=59 * 1024 * 1024
        ),
    )(prev_field, curr_field, coefficient, recordings, receivers, image_in)
    return pl.pallas_call(
        write_out,
        out_shape=(jax.ShapeDtypeStruct(curr_field.shape, f32), jax.ShapeDtypeStruct(image, f32)),
        in_specs=[vmem, vmem],
        out_specs=(anywhere, anywhere),
        scratch_shapes=[dma((9,))],
        compiler_params=pltpu.CompilerParams(vmem_limit_bytes=1024 * 1024),
    )(pltpu.with_memory_space_constraint(field, pltpu.VMEM), pltpu.with_memory_space_constraint(image_out, pltpu.VMEM))


def solution(mesh):
    placed = (
        P("group", "space", None, None),
        P("group", "space", None, None),
        P("space", None, None),
        P("group", None, None),
        P("group", None),
        P("space", "group", None),
    )
    return jax.shard_map(
        on_device,
        mesh=mesh,
        in_specs=placed,
        out_specs=(P("group", "space", None, None), P("space", "group", None)),
        check_vma=False,
    )
```

```python
import jax
import jax.numpy as jnp
from jax import lax
from jax.experimental import pallas as pl
from jax.experimental.pallas import tpu as pltpu
from jax.sharding import PartitionSpec as P

SCALE = 5040.0
TAPS = (8064.0, -1008.0, 128.0, -9.0)
CENTRE = 3.0 * -14350.0
PAD = 4
CHUNKS = 8
ROWS = 4
BLOCK = 32
NT = (((1,), (1,)), ((), ()))


def dot(a, b):
    return jnp.dot(a, b, preferred_element_type=jnp.float32)


def dot_nt(a, b):
    return lax.dot_general(a, b, NT, preferred_element_type=jnp.float32)


def split2(v):
    high = v.astype(jnp.bfloat16)
    return high, (v - high.astype(jnp.float32)).astype(jnp.bfloat16)


def iota(shape, dim):
    return lax.broadcasted_iota(jnp.int32, shape, dim)


def kernel(
    prev_hbm, curr_hbm, coef_hbm, rec_ref, idx_ref, image_ref,
    field, image_out,
    older, newer, coef, far, near, relay, mixed, band, amounts, early, late, from_x, from_z, from_late, away_late, from_late_z,
    load_sem, far_send, far_recv, near_send, near_recv, via_recv, pass_send,
    x_send, x_recv, z_send, z_recv, late_send, late_recv, late_z_send, late_z_recv,
):
    depth, nx, ny = coef.shape
    rows = nx // CHUNKS
    slabs = lax.axis_size("space")
    group = lax.axis_index("group")
    slab = lax.axis_index("space")
    my_x, my_z = group // 2, lax.rem(group, 2)
    core = lax.rem(slab, 2)
    far_slab, near_slab = slab - 1 + 2 * core, slab + 1 - 2 * core
    has_far = (slab > 0) & (slab < slabs - 1)
    far_start, near_start = core * (depth - PAD), (1 - core) * (depth - PAD)

    row, place = slab // 4, lax.rem(slab, 4)
    corner = (place == 0) | (place == 3)
    turn = 1 - 2 * core
    by_relay = jnp.where(corner, core * (2 * ROWS - 2 - 2 * row) + (1 - core) * 2 * row, 0)
    relayed = jnp.where(corner, (1 - core) * (2 * ROWS - 2 - 2 * row) + core * 2 * row, 0)
    partner, onward, behind = slab + 3 * turn, slab + 4 * turn, slab - 4 * turn
    has_onward = corner & (onward >= 0) & (onward < slabs)
    has_behind = corner & (behind >= 0) & (behind < slabs)

    def plane(p):
        return p + core * (depth - 1 - 2 * p)

    loads = [
        pltpu.make_async_copy(curr_hbm.at[0], newer.at[pl.ds(PAD, depth)], load_sem.at[0]),
        pltpu.make_async_copy(coef_hbm, coef, load_sem.at[1]),
        pltpu.make_async_copy(prev_hbm.at[0], older.at[pl.ds(PAD, depth)], load_sem.at[2]),
    ]
    for load in loads:
        load.start()

    barrier = pltpu.get_barrier_semaphore()

    def greet(there, slab_id):
        @pl.when(there)
        def _():
            pl.semaphore_signal(barrier, inc=1, device_id={"space": slab_id})

    pl.semaphore_signal(barrier, inc=1, device_id={"group": my_x * 2 + 1 - my_z})
    for hop in (2, 1, 3):
        pl.semaphore_signal(barrier, inc=1, device_id={"group": lax.rem(my_x + hop, 4) * 2 + my_z})
    greet(corner, partner)
    greet(has_onward, onward)
    greet(has_behind, behind)
    greet(has_far, far_slab)
    pl.semaphore_signal(barrier, inc=1, device_id={"space": near_slab})
    pl.semaphore_wait(barrier, 5 + sum(there.astype(jnp.int32) for there in (has_far, corner, has_onward, has_behind)))

    def chunk_of(i):
        return lax.rem(my_x + 1 + i, 4) * 2 + lax.rem(my_z + 1 + i // 4, 2)

    def rows_of(i):
        return pl.ds(pl.multiple_of(chunk_of(i) * rows, rows), rows)

    def face(step, i):
        if step == 0:
            return curr_hbm.at[0, pl.ds(far_start, PAD), rows_of(i)]
        return older.at[pl.ds(PAD + far_start, PAD), rows_of(i)]

    def far_copy(step, i):
        return pltpu.make_async_remote_copy(
            face(step, i), far.at[step, :, rows_of(i)], far_send.at[step, i], far_recv.at[step, i],
            device_id={"space": far_slab},
        )

    def via_copy(step, i):
        return pltpu.make_async_remote_copy(
            face(step, i), relay.at[step, :, rows_of(i)], far_send.at[step, i], via_recv.at[step, i],
            device_id={"space": partner},
        )

    def pass_copy(step, i):
        return pltpu.make_async_remote_copy(
            relay.at[step, :, rows_of(i)], far.at[step, :, rows_of(i)], pass_send.at[step, i], far_recv.at[step, i],
            device_id={"space": onward},
        )

    def order(m):
        return lax.rem(m + core * (CHUNKS - by_relay), CHUNKS)

    def partner_order(m):
        return lax.rem(m + (1 - core) * (CHUNKS - relayed), CHUNKS)

    def send_far(step, m):
        @pl.when(m < by_relay)
        def _():
            via_copy(step, order(m)).start()

        @pl.when(m >= by_relay)
        def _():
            far_copy(step, order(m)).start()

    def pass_on(step, first, count):
        for m in range(count):
            @pl.when(first + m < relayed)
            def _():
                via_copy(step, partner_order(first + m)).wait_recv()
                pass_copy(step, partner_order(first + m)).start()

    def near_copy(step):
        source = curr_hbm.at[0, pl.ds(near_start, PAD)] if step == 0 else older.at[pl.ds(PAD + near_start, PAD)]
        return pltpu.make_async_remote_copy(
            source, near.at[step], near_send.at[step], near_recv.at[step], device_id={"space": near_slab}
        )

    @pl.when(has_far)
    def _():
        @pl.loop(0, CHUNKS)
        def _(i):
            send_far(0, i)

    near_copy(0).start()

    for ref in (older, newer):
        zero = jnp.zeros((PAD, nx, ny), jnp.float32)
        ref[pl.ds(0, PAD)] = zero
        ref[pl.ds(PAD + depth, PAD)] = zero
    apart = jnp.abs(iota((nx, nx), 0) - iota((nx, nx), 1))
    matrix = jnp.zeros((nx, nx), jnp.float32)
    for j, tap in enumerate(TAPS):
        matrix = jnp.where(apart == j + 1, tap, matrix)
    band[...] = matrix.astype(jnp.bfloat16)
    index = idx_ref[...]
    receivers = index.shape[1]
    at_y = iota((ny, receivers), 0) == (index & (ny - 1))
    for step in range(2):
        high, low = split2(rec_ref[0, pl.ds(step, 1), :] * SCALE)
        amounts[step, 0] = jnp.where(at_y, high.astype(jnp.float32), 0.0).astype(jnp.bfloat16)
        amounts[step, 1] = jnp.where(at_y, low.astype(jnp.float32), 0.0).astype(jnp.bfloat16)

    for load in loads:
        load.wait()

    def mix(step, field_ref, z):
        value = field_ref[pl.ds(z + PAD, PAD)].reshape(PAD * nx, ny)
        high, low = split2(value)
        along_y = dot(high, band[...]) + dot(low, band[...])
        beside = [jnp.concatenate([v[k * nx : (k + 1) * nx] for k in range(PAD)], axis=1) for v in (high, low)]
        along_x = dot(band[...], beside[0]) + dot(band[...], beside[1])
        at_row = iota((PAD * nx, receivers), 0) + (slab * depth + z) * nx == (index >> 8)
        onehot = jnp.where(at_row, 1.0, 0.0).astype(jnp.bfloat16)
        injected = dot_nt(onehot, amounts[step, 0]) + dot_nt(onehot, amounts[step, 1])
        for k in range(PAD):
            mixed[z + k] = (along_y + injected)[k * nx : (k + 1) * nx] + along_x[:, k * ny : (k + 1) * ny]

    def update(z, field_ref, old_ref, old_pad, new_ref, new_pad):
        @pl.loop(0, nx // BLOCK)
        def _(b):
            part = pl.ds(pl.multiple_of(b * BLOCK, BLOCK), BLOCK)
            window = [field_ref[z + k, part] for k in range(3 * PAD)]
            for k in range(PAD):
                centre = window[k + PAD]
                total = CENTRE * centre + mixed[z + k, part]
                for j, tap in enumerate(TAPS):
                    total += tap * (window[k + PAD + j + 1] + window[k + PAD - j - 1])
                new_ref[z + k + new_pad, part] = (
                    2.0 * centre - old_ref[z + k + old_pad, part] + (coef[z + k, part] * (1.0 / SCALE)) * total
                )

    quads = depth // PAD

    def quad(g):
        return pl.multiple_of((g + core * (quads - 1 - 2 * g)) * PAD, PAD)

    @pl.loop(0, quads)
    def _(g):
        mix(0, newer, g * PAD)
        update(g * PAD, newer, older, PAD, older, PAD)

    def add_halo(h, z_of, target, pad, part):
        for k in range(PAD):
            total = TAPS[k] * h(0, part)
            for j in range(k + 1, PAD):
                total += TAPS[j] * h(j - k, part)
            z = z_of(k)
            target[z + pad, part] += (coef[z, part] * (1.0 / SCALE)) * total

    def add_near(step, target, pad):
        near_copy(step).wait_recv()

        @pl.loop(0, nx // BLOCK)
        def _(b):
            add_halo(
                lambda k, part: near[step, k + core * (PAD - 1 - 2 * k), part],
                lambda k: plane(depth - 1 - k),
                target, pad, pl.ds(pl.multiple_of(b * BLOCK, BLOCK), BLOCK),
            )

    def add_far(step, i, target, pad):
        far_copy(step, i).wait_recv()
        add_halo(
            lambda k, part: far[step, (PAD - 1 - k) + core * (2 * k - PAD + 1), part],
            plane, target, pad, rows_of(i),
        )

    add_near(0, older, PAD)
    near_copy(1).start()

    @pl.loop(1, quads)
    def _(g):
        mix(1, older, quad(g))
        pass_on(0, 2 * g - 2, 2)

    @pl.loop(2, quads)
    def _(g):
        update(quad(g), older, newer, PAD, field.at[0], 0)

    @pl.when(has_far)
    def _():
        @pl.loop(0, CHUNKS)
        def _(i):
            add_far(0, order(i), older, PAD)
            send_far(1, i)

    mix(1, older, quad(0))

    @pl.loop(0, 2)
    def _(g):
        update(quad(g), older, newer, PAD, field.at[0], 0)

    add_near(1, field.at[0], 0)

    half = rows // 2
    even = jnp.where(iota((ny // 2, ny), 1) == 2 * iota((ny // 2, ny), 0), 1.0, 0.0).astype(jnp.bfloat16)

    def terms_of(planes):
        size = planes[0].shape[0]
        value = jnp.concatenate(planes, axis=0)
        pieces = []
        for _ in range(3):
            pieces.append(value.astype(jnp.bfloat16))
            value = value - pieces[-1].astype(jnp.float32)
        columns = dot_nt(jnp.concatenate(pieces, axis=0), even).astype(jnp.bfloat16)
        count = 3 * len(planes)
        columns = jnp.concatenate([columns[n * size : (n + 1) * size] for n in range(count)], axis=1)
        picked = dot(even[: size // 2, :size], columns)
        width = ny // 2
        result = []
        for k in range(len(planes)):
            one, two, three = (picked[:, (k + p * len(planes)) * width :][:, :width] for p in range(3))
            sample = one + two + three
            result.append(jnp.log(1.0 + sample * sample))
        return result

    count = PAD // 2
    first_early, first_late = (1 - core) * count, core * (depth // 2 - count)

    @pl.loop(0, depth // 2 - count, step=2)
    def _(q):
        for k, term in enumerate(terms_of([field[0, 2 * (first_early + q + k)] for k in range(2)])):
            early[:, q + k] = term.reshape(CHUNKS, half, ny // 2)

    def to_x(hop, which):
        other = lax.rem(my_x + hop, 4)
        return pltpu.make_async_remote_copy(
            early.at[other * 2 + which], from_x.at[which, hop - 1], x_send.at[which, hop - 1], x_recv.at[which, hop - 1],
            device_id={"group": other * 2 + my_z},
        )

    away, mine = my_x * 2 + 1 - my_z, group
    to_z = pltpu.make_async_remote_copy(early.at[away], from_z, z_send, z_recv, device_id={"group": away})

    @pl.loop(0, 6)
    def _(n):
        to_x(1 + n // 2, lax.rem(n, 2)).start()

    def sum_x(which):
        total = early[my_x * 2 + which]
        for hop in range(1, 4):
            to_x(hop, which).wait_recv()
            total += from_x[which, hop - 1]
        return total

    def late_terms(i):
        @pl.when(has_far)
        def _():
            add_far(1, i, field.at[0], 0)

        part = rows_of(i)
        return terms_of([field[0, 2 * (first_late + q), part] for q in range(count)])

    def to_owner(i):
        return pltpu.make_async_remote_copy(
            late.at[i], from_late.at[i], late_send.at[i], late_recv.at[i],
            device_id={"group": lax.rem(my_x + 1 + i, 4) * 2 + my_z},
        )

    def late_chunk(i):
        for q, term in enumerate(late_terms(i)):
            late[i, q] = term

        @pl.when(i != 3)
        def _():
            to_owner(i).start()

    pass_on(1, 0, 2 * ROWS - 2)

    @pl.loop(0, 2)
    def _(i):
        late_chunk(i)

    early[away] = sum_x(1 - my_z)
    to_z.start()
    early[mine] = sum_x(my_z)

    @pl.loop(2, 5)
    def _(i):
        late_chunk(i)

    late_to_z = pltpu.make_async_remote_copy(
        away_late, from_late_z, late_z_send, late_z_recv, device_id={"group": away}
    )
    for i in range(3):
        to_owner(i).wait_recv()
    away_late[...] = late[3] + (from_late[0] + from_late[1] + from_late[2])
    late_to_z.start()

    @pl.loop(5, CHUNKS - 1)
    def _(i):
        late_chunk(i)

    to_z.wait_recv()
    at_early = pl.ds(first_early, depth // 2 - count)
    image_out[at_early] = image_ref[at_early] + (jnp.exp((early[mine] + from_z[...]) * 0.125) - 1.0)
    last = late_terms(CHUNKS - 1)
    for i in range(4, CHUNKS - 1):
        to_owner(i).wait_recv()
    late_to_z.wait_recv()
    for q in range(count):
        total = last[q] + (from_late[4, q] + from_late[5, q]) + (from_late[6, q] + from_late_z[q])
        image_out[first_late + q] = image_ref[first_late + q] + (jnp.exp(total * 0.125) - 1.0)

    late_to_z.wait_send()
    to_z.wait_send()
    for step in range(2):
        near_copy(step).wait_send()

    @pl.loop(0, 6)
    def _(n):
        to_x(1 + n // 2, lax.rem(n, 2)).wait_send()

    @pl.loop(0, CHUNKS - 1)
    def _(i):
        @pl.when(i != 3)
        def _():
            to_owner(i).wait_send()

    for step in range(2):
        @pl.loop(0, relayed)
        def _(i):
            pass_copy(step, partner_order(i)).wait_send()

    @pl.when(has_far)
    def _():
        @pl.loop(0, CHUNKS)
        def _(i):
            for step in range(2):
                far_copy(step, i).wait_send()


def write_out(field, image, field_hbm, image_hbm, sems):
    parts = sems.shape[0] - 1
    planes = field.shape[1] // parts
    copies = [
        pltpu.make_async_copy(field.at[:, pl.ds(i * planes, planes)], field_hbm.at[:, pl.ds(i * planes, planes)], sems.at[i])
        for i in range(parts)
    ]
    copies.append(pltpu.make_async_copy(image, image_hbm, sems.at[parts]))
    for copy in copies:
        copy.start()
    for copy in copies:
        copy.wait()


def on_device(prev_field, curr_field, coefficient, recordings, receivers, image_in):
    depth, nx, ny = coefficient.shape
    _, steps, count = recordings.shape
    padded = (depth + 2 * PAD, nx, ny)
    image = image_in.shape
    early, late = (image[0] - PAD // 2,) + image[1:], (PAD // 2,) + image[1:]
    anywhere = pl.BlockSpec(memory_space=pl.ANY)
    vmem = pl.BlockSpec(memory_space=pltpu.VMEM)
    dma = pltpu.SemaphoreType.DMA
    f32 = jnp.float32
    field, image_out = pl.pallas_call(
        kernel,
        out_shape=(pltpu.VMEM(curr_field.shape, f32), pltpu.VMEM(image, f32)),
        in_specs=[anywhere, anywhere, anywhere, vmem, vmem, vmem],
        out_specs=(vmem, vmem),
        scratch_shapes=[
            pltpu.VMEM(padded, f32),
            pltpu.VMEM(padded, f32),
            pltpu.VMEM((depth, nx, ny), f32),
            pltpu.VMEM((steps, PAD, nx, ny), f32),
            pltpu.VMEM((steps, PAD, nx, ny), f32),
            pltpu.VMEM((steps, PAD, nx, ny), f32),
            pltpu.VMEM((depth, nx, ny), f32),
            pltpu.VMEM((nx, nx), jnp.bfloat16),
            pltpu.VMEM((steps, 2, ny, count), jnp.bfloat16),
            pltpu.VMEM((CHUNKS,) + early, f32),
            pltpu.VMEM((CHUNKS - 1,) + late, f32),
            pltpu.VMEM((2, 3) + early, f32),
            pltpu.VMEM(early, f32),
            pltpu.VMEM((CHUNKS - 1,) + late, f32),
            pltpu.VMEM(late, f32),
            pltpu.VMEM(late, f32),
            dma((3,)), dma((steps, CHUNKS)), dma((steps, CHUNKS)), dma((steps,)), dma((steps,)),
            dma((steps, CHUNKS)), dma((steps, CHUNKS)),
            dma((2, 3)), dma((2, 3)), dma, dma, dma((CHUNKS - 1,)), dma((CHUNKS - 1,)), dma, dma,
        ],
        compiler_params=pltpu.CompilerParams(
            collective_id=0, has_side_effects=True, vmem_limit_bytes=59 * 1024 * 1024
        ),
    )(prev_field, curr_field, coefficient, recordings, receivers, image_in)
    return pl.pallas_call(
        write_out,
        out_shape=(jax.ShapeDtypeStruct(curr_field.shape, f32), jax.ShapeDtypeStruct(image, f32)),
        in_specs=[vmem, vmem],
        out_specs=(anywhere, anywhere),
        scratch_shapes=[dma((9,))],
        compiler_params=pltpu.CompilerParams(vmem_limit_bytes=1024 * 1024),
    )(pltpu.with_memory_space_constraint(field, pltpu.VMEM), pltpu.with_memory_space_constraint(image_out, pltpu.VMEM))


def solution(mesh):
    placed = (
        P("group", "space", None, None),
        P("group", "space", None, None),
        P("space", None, None),
        P("group", None, None),
        P("group", None),
        P("space", "group", None),
    )
    return jax.shard_map(
        on_device,
        mesh=mesh,
        in_specs=placed,
        out_specs=(P("group", "space", None, None), P("space", "group", None)),
        check_vma=False,
    )
```

```python
import jax
import jax.numpy as jnp
from jax import lax
from jax.experimental import pallas as pl
from jax.experimental.pallas import tpu as pltpu
from jax.sharding import PartitionSpec as P

SCALE = 5040.0
TAPS = (8064.0, -1008.0, 128.0, -9.0)
CENTRE = 3.0 * -14350.0
PAD = 4
CHUNKS = 8
ROWS = 4
BLOCK = 32
NT = (((1,), (1,)), ((), ()))


def dot(a, b):
    return jnp.dot(a, b, preferred_element_type=jnp.float32)


def dot_nt(a, b):
    return lax.dot_general(a, b, NT, preferred_element_type=jnp.float32)


def split2(v):
    high = v.astype(jnp.bfloat16)
    return high, (v - high.astype(jnp.float32)).astype(jnp.bfloat16)


def iota(shape, dim):
    return lax.broadcasted_iota(jnp.int32, shape, dim)


def kernel(
    prev_hbm, curr_hbm, coef_hbm, rec_ref, idx_ref, image_ref,
    field, image_out,
    older, newer, coef, far, near, relay, mixed, band, amounts, early, late, from_x, from_z, from_late, away_late, from_late_z,
    load_sem, far_send, far_recv, near_send, near_recv, via_recv, pass_send,
    x_send, x_recv, z_send, z_recv, late_send, late_recv, late_z_send, late_z_recv,
):
    depth, nx, ny = coef.shape
    rows = nx // CHUNKS
    slabs = lax.axis_size("space")
    group = lax.axis_index("group")
    slab = lax.axis_index("space")
    my_x, my_z = group // 2, lax.rem(group, 2)
    core = lax.rem(slab, 2)
    far_slab, near_slab = slab - 1 + 2 * core, slab + 1 - 2 * core
    has_far = (slab > 0) & (slab < slabs - 1)
    far_start, near_start = core * (depth - PAD), (1 - core) * (depth - PAD)

    row, place = slab // 4, lax.rem(slab, 4)
    corner = (place == 0) | (place == 3)
    turn = 1 - 2 * core
    by_relay = jnp.where(corner, core * (2 * ROWS - 2 - 2 * row) + (1 - core) * 2 * row, 0)
    relayed = jnp.where(corner, (1 - core) * (2 * ROWS - 2 - 2 * row) + core * 2 * row, 0)
    partner, onward, behind = slab + 3 * turn, slab + 4 * turn, slab - 4 * turn
    has_onward = corner & (onward >= 0) & (onward < slabs)
    has_behind = corner & (behind >= 0) & (behind < slabs)

    def plane(p):
        return p + core * (depth - 1 - 2 * p)

    loads = [
        pltpu.make_async_copy(curr_hbm.at[0], newer.at[pl.ds(PAD, depth)], load_sem.at[0]),
        pltpu.make_async_copy(coef_hbm, coef, load_sem.at[1]),
        pltpu.make_async_copy(prev_hbm.at[0], older.at[pl.ds(PAD, depth)], load_sem.at[2]),
    ]
    for load in loads:
        load.start()

    barrier = pltpu.get_barrier_semaphore()

    def greet(there, slab_id):
        @pl.when(there)
        def _():
            pl.semaphore_signal(barrier, inc=1, device_id={"space": slab_id})

    pl.semaphore_signal(barrier, inc=1, device_id={"group": my_x * 2 + 1 - my_z})
    for hop in (2, 1, 3):
        pl.semaphore_signal(barrier, inc=1, device_id={"group": lax.rem(my_x + hop, 4) * 2 + my_z})
    greet(corner, partner)
    greet(has_onward, onward)
    greet(has_behind, behind)
    greet(has_far, far_slab)
    pl.semaphore_signal(barrier, inc=1, device_id={"space": near_slab})
    pl.semaphore_wait(barrier, 5 + sum(there.astype(jnp.int32) for there in (has_far, corner, has_onward, has_behind)))

    def chunk_of(i):
        return lax.rem(my_x + 1 + i, 4) * 2 + lax.rem(my_z + 1 + i // 4, 2)

    def rows_of(i):
        return pl.ds(pl.multiple_of(chunk_of(i) * rows, rows), rows)

    def face(step, i):
        if step == 0:
            return curr_hbm.at[0, pl.ds(far_start, PAD), rows_of(i)]
        return older.at[pl.ds(PAD + far_start, PAD), rows_of(i)]

    def far_copy(step, i):
        return pltpu.make_async_remote_copy(
            face(step, i), far.at[step, :, rows_of(i)], far_send.at[step, i], far_recv.at[step, i],
            device_id={"space": far_slab},
        )

    def via_copy(step, i):
        return pltpu.make_async_remote_copy(
            face(step, i), relay.at[step, :, rows_of(i)], far_send.at[step, i], via_recv.at[step, i],
            device_id={"space": partner},
        )

    def pass_copy(step, i):
        return pltpu.make_async_remote_copy(
            relay.at[step, :, rows_of(i)], far.at[step, :, rows_of(i)], pass_send.at[step, i], far_recv.at[step, i],
            device_id={"space": onward},
        )

    def order(m):
        return lax.rem(m + core * (CHUNKS - by_relay), CHUNKS)

    def partner_order(m):
        return lax.rem(m + (1 - core) * (CHUNKS - relayed), CHUNKS)

    def send_far(step, m):
        @pl.when(m < by_relay)
        def _():
            via_copy(step, order(m)).start()

        @pl.when(m >= by_relay)
        def _():
            far_copy(step, order(m)).start()

    def pass_on(step, first, count):
        for m in range(count):
            @pl.when(first + m < relayed)
            def _():
                via_copy(step, partner_order(first + m)).wait_recv()
                pass_copy(step, partner_order(first + m)).start()

    def near_copy(step):
        source = curr_hbm.at[0, pl.ds(near_start, PAD)] if step == 0 else older.at[pl.ds(PAD + near_start, PAD)]
        return pltpu.make_async_remote_copy(
            source, near.at[step], near_send.at[step], near_recv.at[step], device_id={"space": near_slab}
        )

    @pl.when(has_far)
    def _():
        @pl.loop(0, CHUNKS)
        def _(i):
            send_far(0, i)

    near_copy(0).start()

    for ref in (older, newer):
        zero = jnp.zeros((PAD, nx, ny), jnp.float32)
        ref[pl.ds(0, PAD)] = zero
        ref[pl.ds(PAD + depth, PAD)] = zero
    apart = jnp.abs(iota((nx, nx), 0) - iota((nx, nx), 1))
    matrix = jnp.zeros((nx, nx), jnp.float32)
    for j, tap in enumerate(TAPS):
        matrix = jnp.where(apart == j + 1, tap, matrix)
    band[...] = matrix.astype(jnp.bfloat16)
    index = idx_ref[...]
    receivers = index.shape[1]
    at_y = iota((ny, receivers), 0) == (index & (ny - 1))
    for step in range(2):
        high, low = split2(rec_ref[0, pl.ds(step, 1), :] * SCALE)
        amounts[step, 0] = jnp.where(at_y, high.astype(jnp.float32), 0.0).astype(jnp.bfloat16)
        amounts[step, 1] = jnp.where(at_y, low.astype(jnp.float32), 0.0).astype(jnp.bfloat16)

    for load in loads:
        load.wait()

    def mix(step, field_ref, z):
        value = field_ref[pl.ds(z + PAD, PAD)].reshape(PAD * nx, ny)
        high, low = split2(value)
        along_y = dot(high, band[...]) + dot(low, band[...])
        beside = [jnp.concatenate([v[k * nx : (k + 1) * nx] for k in range(PAD)], axis=1) for v in (high, low)]
        along_x = dot(band[...], beside[0]) + dot(band[...], beside[1])
        at_row = iota((PAD * nx, receivers), 0) + (slab * depth + z) * nx == (index >> 8)
        onehot = jnp.where(at_row, 1.0, 0.0).astype(jnp.bfloat16)
        injected = dot_nt(onehot, amounts[step, 0]) + dot_nt(onehot, amounts[step, 1])
        for k in range(PAD):
            mixed[z + k] = (along_y + injected)[k * nx : (k + 1) * nx] + along_x[:, k * ny : (k + 1) * ny]

    def update(z, field_ref, old_ref, old_pad, new_ref, new_pad):
        @pl.loop(0, nx // BLOCK)
        def _(b):
            part = pl.ds(pl.multiple_of(b * BLOCK, BLOCK), BLOCK)
            window = [field_ref[z + k, part] for k in range(3 * PAD)]
            for k in range(PAD):
                centre = window[k + PAD]
                total = CENTRE * centre + mixed[z + k, part]
                for j, tap in enumerate(TAPS):
                    total += tap * (window[k + PAD + j + 1] + window[k + PAD - j - 1])
                new_ref[z + k + new_pad, part] = (
                    2.0 * centre - old_ref[z + k + old_pad, part] + (coef[z + k, part] * (1.0 / SCALE)) * total
                )

    quads = depth // PAD

    def quad(g):
        return pl.multiple_of((g + core * (quads - 1 - 2 * g)) * PAD, PAD)

    @pl.loop(0, quads)
    def _(g):
        mix(0, newer, g * PAD)
        update(g * PAD, newer, older, PAD, older, PAD)

    def add_halo(h, z_of, target, pad, part):
        for k in range(PAD):
            total = TAPS[k] * h(0, part)
            for j in range(k + 1, PAD):
                total += TAPS[j] * h(j - k, part)
            z = z_of(k)
            target[z + pad, part] += (coef[z, part] * (1.0 / SCALE)) * total

    def add_near(step, target, pad):
        near_copy(step).wait_recv()

        @pl.loop(0, nx // BLOCK)
        def _(b):
            add_halo(
                lambda k, part: near[step, k + core * (PAD - 1 - 2 * k), part],
                lambda k: plane(depth - 1 - k),
                target, pad, pl.ds(pl.multiple_of(b * BLOCK, BLOCK), BLOCK),
            )

    def add_far(step, i, target, pad):
        far_copy(step, i).wait_recv()
        add_halo(
            lambda k, part: far[step, (PAD - 1 - k) + core * (2 * k - PAD + 1), part],
            plane, target, pad, rows_of(i),
        )

    add_near(0, older, PAD)
    near_copy(1).start()

    @pl.loop(1, quads)
    def _(g):
        mix(1, older, quad(g))
        pass_on(0, 2 * g - 2, 2)

    @pl.loop(2, quads)
    def _(g):
        update(quad(g), older, newer, PAD, field.at[0], 0)

    @pl.when(has_far)
    def _():
        @pl.loop(0, CHUNKS)
        def _(i):
            add_far(0, order(i), older, PAD)
            send_far(1, i)

    mix(1, older, quad(0))

    @pl.loop(0, 2)
    def _(g):
        update(quad(g), older, newer, PAD, field.at[0], 0)

    add_near(1, field.at[0], 0)

    half = rows // 2
    even = jnp.where(iota((ny // 2, ny), 1) == 2 * iota((ny // 2, ny), 0), 1.0, 0.0).astype(jnp.bfloat16)

    def terms_of(planes):
        size = planes[0].shape[0]
        value = jnp.concatenate(planes, axis=0)
        pieces = []
        for _ in range(3):
            pieces.append(value.astype(jnp.bfloat16))
            value = value - pieces[-1].astype(jnp.float32)
        columns = dot_nt(jnp.concatenate(pieces, axis=0), even).astype(jnp.bfloat16)
        count = 3 * len(planes)
        columns = jnp.concatenate([columns[n * size : (n + 1) * size] for n in range(count)], axis=1)
        picked = dot(even[: size // 2, :size], columns)
        width = ny // 2
        result = []
        for k in range(len(planes)):
            one, two, three = (picked[:, (k + p * len(planes)) * width :][:, :width] for p in range(3))
            sample = one + two + three
            result.append(jnp.log(1.0 + sample * sample))
        return result

    count = PAD // 2
    first_early, first_late = (1 - core) * count, core * (depth // 2 - count)

    @pl.loop(0, depth // 2 - count, step=2)
    def _(q):
        for k, term in enumerate(terms_of([field[0, 2 * (first_early + q + k)] for k in range(2)])):
            early[:, q + k] = term.reshape(CHUNKS, half, ny // 2)

    def to_x(hop, which):
        other = lax.rem(my_x + hop, 4)
        return pltpu.make_async_remote_copy(
            early.at[other * 2 + which], from_x.at[which, hop - 1], x_send.at[which, hop - 1], x_recv.at[which, hop - 1],
            device_id={"group": other * 2 + my_z},
        )

    away, mine = my_x * 2 + 1 - my_z, group
    to_z = pltpu.make_async_remote_copy(early.at[away], from_z, z_send, z_recv, device_id={"group": away})

    @pl.loop(0, 6)
    def _(n):
        to_x(1 + n // 2, lax.rem(n, 2)).start()

    def sum_x(which):
        total = early[my_x * 2 + which]
        for hop in range(1, 4):
            to_x(hop, which).wait_recv()
            total += from_x[which, hop - 1]
        return total

    def late_terms(i):
        @pl.when(has_far)
        def _():
            add_far(1, i, field.at[0], 0)

        part = rows_of(i)
        return terms_of([field[0, 2 * (first_late + q), part] for q in range(count)])

    def to_owner(i):
        return pltpu.make_async_remote_copy(
            late.at[i], from_late.at[i], late_send.at[i], late_recv.at[i],
            device_id={"group": lax.rem(my_x + 1 + i, 4) * 2 + my_z},
        )

    def late_chunk(i):
        for q, term in enumerate(late_terms(i)):
            late[i, q] = term

        @pl.when(i != 3)
        def _():
            to_owner(i).start()

        @pl.when(jnp.logical_not(has_far))
        def _():
            pass_on(1, i, 1)

    @pl.when(has_far)
    def _():
        pass_on(1, 0, 2 * ROWS - 2)

    @pl.loop(0, 2)
    def _(i):
        late_chunk(i)

    @pl.loop(2, 5)
    def _(i):
        late_chunk(i)

    late_to_z = pltpu.make_async_remote_copy(
        away_late, from_late_z, late_z_send, late_z_recv, device_id={"group": away}
    )
    early[away] = sum_x(1 - my_z)
    to_z.start()
    early[mine] = sum_x(my_z)

    for i in range(3):
        to_owner(i).wait_recv()
    away_late[...] = late[3] + (from_late[0] + from_late[1] + from_late[2])
    late_to_z.start()

    @pl.loop(5, CHUNKS - 1)
    def _(i):
        late_chunk(i)

    to_z.wait_recv()
    at_early = pl.ds(first_early, depth // 2 - count)
    image_out[at_early] = image_ref[at_early] + (jnp.exp((early[mine] + from_z[...]) * 0.125) - 1.0)
    last = late_terms(CHUNKS - 1)
    for i in range(4, CHUNKS - 1):
        to_owner(i).wait_recv()
    late_to_z.wait_recv()
    for q in range(count):
        total = last[q] + (from_late[4, q] + from_late[5, q]) + (from_late[6, q] + from_late_z[q])
        image_out[first_late + q] = image_ref[first_late + q] + (jnp.exp(total * 0.125) - 1.0)

    late_to_z.wait_send()
    to_z.wait_send()
    for step in range(2):
        near_copy(step).wait_send()

    @pl.loop(0, 6)
    def _(n):
        to_x(1 + n // 2, lax.rem(n, 2)).wait_send()

    @pl.loop(0, CHUNKS - 1)
    def _(i):
        @pl.when(i != 3)
        def _():
            to_owner(i).wait_send()

    for step in range(2):
        @pl.loop(0, relayed)
        def _(i):
            pass_copy(step, partner_order(i)).wait_send()

    @pl.when(has_far)
    def _():
        @pl.loop(0, CHUNKS)
        def _(i):
            for step in range(2):
                far_copy(step, i).wait_send()


def write_out(field, image, field_hbm, image_hbm, sems):
    parts = sems.shape[0] - 1
    planes = field.shape[1] // parts
    copies = [
        pltpu.make_async_copy(field.at[:, pl.ds(i * planes, planes)], field_hbm.at[:, pl.ds(i * planes, planes)], sems.at[i])
        for i in range(parts)
    ]
    copies.append(pltpu.make_async_copy(image, image_hbm, sems.at[parts]))
    for copy in copies:
        copy.start()
    for copy in copies:
        copy.wait()


def on_device(prev_field, curr_field, coefficient, recordings, receivers, image_in):
    depth, nx, ny = coefficient.shape
    _, steps, count = recordings.shape
    padded = (depth + 2 * PAD, nx, ny)
    image = image_in.shape
    early, late = (image[0] - PAD // 2,) + image[1:], (PAD // 2,) + image[1:]
    anywhere = pl.BlockSpec(memory_space=pl.ANY)
    vmem = pl.BlockSpec(memory_space=pltpu.VMEM)
    dma = pltpu.SemaphoreType.DMA
    f32 = jnp.float32
    field, image_out = pl.pallas_call(
        kernel,
        out_shape=(pltpu.VMEM(curr_field.shape, f32), pltpu.VMEM(image, f32)),
        in_specs=[anywhere, anywhere, anywhere, vmem, vmem, vmem],
        out_specs=(vmem, vmem),
        scratch_shapes=[
            pltpu.VMEM(padded, f32),
            pltpu.VMEM(padded, f32),
            pltpu.VMEM((depth, nx, ny), f32),
            pltpu.VMEM((steps, PAD, nx, ny), f32),
            pltpu.VMEM((steps, PAD, nx, ny), f32),
            pltpu.VMEM((steps, PAD, nx, ny), f32),
            pltpu.VMEM((depth, nx, ny), f32),
            pltpu.VMEM((nx, nx), jnp.bfloat16),
            pltpu.VMEM((steps, 2, ny, count), jnp.bfloat16),
            pltpu.VMEM((CHUNKS,) + early, f32),
            pltpu.VMEM((CHUNKS - 1,) + late, f32),
            pltpu.VMEM((2, 3) + early, f32),
            pltpu.VMEM(early, f32),
            pltpu.VMEM((CHUNKS - 1,) + late, f32),
            pltpu.VMEM(late, f32),
            pltpu.VMEM(late, f32),
            dma((3,)), dma((steps, CHUNKS)), dma((steps, CHUNKS)), dma((steps,)), dma((steps,)),
            dma((steps, CHUNKS)), dma((steps, CHUNKS)),
            dma((2, 3)), dma((2, 3)), dma, dma, dma((CHUNKS - 1,)), dma((CHUNKS - 1,)), dma, dma,
        ],
        compiler_params=pltpu.CompilerParams(
            collective_id=0, has_side_effects=True, vmem_limit_bytes=59 * 1024 * 1024
        ),
    )(prev_field, curr_field, coefficient, recordings, receivers, image_in)
    return pl.pallas_call(
        write_out,
        out_shape=(jax.ShapeDtypeStruct(curr_field.shape, f32), jax.ShapeDtypeStruct(image, f32)),
        in_specs=[vmem, vmem],
        out_specs=(anywhere, anywhere),
        scratch_shapes=[dma((9,))],
        compiler_params=pltpu.CompilerParams(vmem_limit_bytes=1024 * 1024),
    )(pltpu.with_memory_space_constraint(field, pltpu.VMEM), pltpu.with_memory_space_constraint(image_out, pltpu.VMEM))


def solution(mesh):
    placed = (
        P("group", "space", None, None),
        P("group", "space", None, None),
        P("space", None, None),
        P("group", None, None),
        P("group", None),
        P("space", "group", None),
    )
    return jax.shard_map(
        on_device,
        mesh=mesh,
        in_specs=placed,
        out_specs=(P("group", "space", None, None), P("space", "group", None)),
        check_vma=False,
    )
```

```python
import jax
import jax.numpy as jnp
from jax import lax
from jax.experimental import pallas as pl
from jax.experimental.pallas import tpu as pltpu
from jax.sharding import PartitionSpec as P

SCALE = 5040.0
TAPS = (8064.0, -1008.0, 128.0, -9.0)
CENTRE = 3.0 * -14350.0
PAD = 4
CHUNKS = 8
ROWS = 4
BLOCK = 32
NT = (((1,), (1,)), ((), ()))


def dot(a, b):
    return jnp.dot(a, b, preferred_element_type=jnp.float32)


def dot_nt(a, b):
    return lax.dot_general(a, b, NT, preferred_element_type=jnp.float32)


def split2(v):
    high = v.astype(jnp.bfloat16)
    return high, (v - high.astype(jnp.float32)).astype(jnp.bfloat16)


def iota(shape, dim):
    return lax.broadcasted_iota(jnp.int32, shape, dim)


def kernel(
    prev_hbm, curr_hbm, coef_hbm, rec_ref, idx_ref, image_ref,
    field, image_out,
    older, newer, coef, far, near, relay, mixed, band, amounts, early, late, from_x, from_z, from_late, away_late, from_late_z,
    load_sem, far_send, far_recv, near_send, near_recv, via_recv, pass_send,
    x_send, x_recv, z_send, z_recv, late_send, late_recv, late_z_send, late_z_recv,
):
    depth, nx, ny = coef.shape
    rows = nx // CHUNKS
    slabs = lax.axis_size("space")
    group = lax.axis_index("group")
    slab = lax.axis_index("space")
    my_x, my_z = group // 2, lax.rem(group, 2)
    core = lax.rem(slab, 2)
    far_slab, near_slab = slab - 1 + 2 * core, slab + 1 - 2 * core
    has_far = (slab > 0) & (slab < slabs - 1)
    far_start, near_start = core * (depth - PAD), (1 - core) * (depth - PAD)

    row, place = slab // 4, lax.rem(slab, 4)
    corner = (place == 0) | (place == 3)
    turn = 1 - 2 * core
    by_relay = jnp.where(corner, core * (2 * ROWS - 2 - 2 * row) + (1 - core) * 2 * row, 0)
    relayed = jnp.where(corner, (1 - core) * (2 * ROWS - 2 - 2 * row) + core * 2 * row, 0)
    partner, onward, behind = slab + 3 * turn, slab + 4 * turn, slab - 4 * turn
    has_onward = corner & (onward >= 0) & (onward < slabs)
    has_behind = corner & (behind >= 0) & (behind < slabs)

    def plane(p):
        return p + core * (depth - 1 - 2 * p)

    loads = [
        pltpu.make_async_copy(curr_hbm.at[0], newer.at[pl.ds(PAD, depth)], load_sem.at[0]),
        pltpu.make_async_copy(coef_hbm, coef, load_sem.at[1]),
        pltpu.make_async_copy(prev_hbm.at[0], older.at[pl.ds(PAD, depth)], load_sem.at[2]),
    ]

    barrier = pltpu.get_barrier_semaphore()

    def greet(there, slab_id):
        @pl.when(there)
        def _():
            pl.semaphore_signal(barrier, inc=1, device_id={"space": slab_id})

    pl.semaphore_signal(barrier, inc=1, device_id={"group": my_x * 2 + 1 - my_z})
    for hop in (2, 1, 3):
        pl.semaphore_signal(barrier, inc=1, device_id={"group": lax.rem(my_x + hop, 4) * 2 + my_z})
    greet(corner, partner)
    greet(has_onward, onward)
    greet(has_behind, behind)
    greet(has_far, far_slab)
    pl.semaphore_signal(barrier, inc=1, device_id={"space": near_slab})
    pl.semaphore_wait(barrier, 5 + sum(there.astype(jnp.int32) for there in (has_far, corner, has_onward, has_behind)))

    def chunk_of(i):
        return lax.rem(my_x + 1 + i, 4) * 2 + lax.rem(my_z + 1 + i // 4, 2)

    def rows_of(i):
        return pl.ds(pl.multiple_of(chunk_of(i) * rows, rows), rows)

    def face(step, i):
        if step == 0:
            return curr_hbm.at[0, pl.ds(far_start, PAD), rows_of(i)]
        return older.at[pl.ds(PAD + far_start, PAD), rows_of(i)]

    def far_copy(step, i):
        return pltpu.make_async_remote_copy(
            face(step, i), far.at[step, :, rows_of(i)], far_send.at[step, i], far_recv.at[step, i],
            device_id={"space": far_slab},
        )

    def via_copy(step, i):
        return pltpu.make_async_remote_copy(
            face(step, i), relay.at[step, :, rows_of(i)], far_send.at[step, i], via_recv.at[step, i],
            device_id={"space": partner},
        )

    def pass_copy(step, i):
        return pltpu.make_async_remote_copy(
            relay.at[step, :, rows_of(i)], far.at[step, :, rows_of(i)], pass_send.at[step, i], far_recv.at[step, i],
            device_id={"space": onward},
        )

    def order(m):
        return lax.rem(m + core * (CHUNKS - by_relay), CHUNKS)

    def partner_order(m):
        return lax.rem(m + (1 - core) * (CHUNKS - relayed), CHUNKS)

    def send_far(step, m):
        @pl.when(m < by_relay)
        def _():
            via_copy(step, order(m)).start()

        @pl.when(m >= by_relay)
        def _():
            far_copy(step, order(m)).start()

    def pass_on(step, first, count):
        for m in range(count):
            @pl.when(first + m < relayed)
            def _():
                via_copy(step, partner_order(first + m)).wait_recv()
                pass_copy(step, partner_order(first + m)).start()

    def near_copy(step):
        source = curr_hbm.at[0, pl.ds(near_start, PAD)] if step == 0 else older.at[pl.ds(PAD + near_start, PAD)]
        return pltpu.make_async_remote_copy(
            source, near.at[step], near_send.at[step], near_recv.at[step], device_id={"space": near_slab}
        )

    @pl.when(has_far)
    def _():
        @pl.loop(0, CHUNKS)
        def _(i):
            send_far(0, i)

    near_copy(0).start()
    for load in loads:
        load.start()

    for ref in (older, newer):
        zero = jnp.zeros((PAD, nx, ny), jnp.float32)
        ref[pl.ds(0, PAD)] = zero
        ref[pl.ds(PAD + depth, PAD)] = zero
    apart = jnp.abs(iota((nx, nx), 0) - iota((nx, nx), 1))
    matrix = jnp.zeros((nx, nx), jnp.float32)
    for j, tap in enumerate(TAPS):
        matrix = jnp.where(apart == j + 1, tap, matrix)
    band[...] = matrix.astype(jnp.bfloat16)
    index = idx_ref[...]
    receivers = index.shape[1]
    at_y = iota((ny, receivers), 0) == (index & (ny - 1))
    for step in range(2):
        high, low = split2(rec_ref[0, pl.ds(step, 1), :] * SCALE)
        amounts[step, 0] = jnp.where(at_y, high.astype(jnp.float32), 0.0).astype(jnp.bfloat16)
        amounts[step, 1] = jnp.where(at_y, low.astype(jnp.float32), 0.0).astype(jnp.bfloat16)

    for load in loads:
        load.wait()

    def mix(step, field_ref, z):
        value = field_ref[pl.ds(z + PAD, PAD)].reshape(PAD * nx, ny)
        high, low = split2(value)
        along_y = dot(high, band[...]) + dot(low, band[...])
        beside = [jnp.concatenate([v[k * nx : (k + 1) * nx] for k in range(PAD)], axis=1) for v in (high, low)]
        along_x = dot(band[...], beside[0]) + dot(band[...], beside[1])
        at_row = iota((PAD * nx, receivers), 0) + (slab * depth + z) * nx == (index >> 8)
        onehot = jnp.where(at_row, 1.0, 0.0).astype(jnp.bfloat16)
        injected = dot_nt(onehot, amounts[step, 0]) + dot_nt(onehot, amounts[step, 1])
        for k in range(PAD):
            mixed[z + k] = (along_y + injected)[k * nx : (k + 1) * nx] + along_x[:, k * ny : (k + 1) * ny]

    def update(z, field_ref, old_ref, old_pad, new_ref, new_pad):
        @pl.loop(0, nx // BLOCK)
        def _(b):
            part = pl.ds(pl.multiple_of(b * BLOCK, BLOCK), BLOCK)
            window = [field_ref[z + k, part] for k in range(3 * PAD)]
            for k in range(PAD):
                centre = window[k + PAD]
                total = CENTRE * centre + mixed[z + k, part]
                for j, tap in enumerate(TAPS):
                    total += tap * (window[k + PAD + j + 1] + window[k + PAD - j - 1])
                new_ref[z + k + new_pad, part] = (
                    2.0 * centre - old_ref[z + k + old_pad, part] + (coef[z + k, part] * (1.0 / SCALE)) * total
                )

    quads = depth // PAD

    def quad(g):
        return pl.multiple_of((g + core * (quads - 1 - 2 * g)) * PAD, PAD)

    @pl.loop(0, quads)
    def _(g):
        mix(0, newer, g * PAD)
        update(g * PAD, newer, older, PAD, older, PAD)

    def add_halo(h, z_of, target, pad, part):
        for k in range(PAD):
            total = TAPS[k] * h(0, part)
            for j in range(k + 1, PAD):
                total += TAPS[j] * h(j - k, part)
            z = z_of(k)
            target[z + pad, part] += (coef[z, part] * (1.0 / SCALE)) * total

    def add_near(step, target, pad):
        near_copy(step).wait_recv()

        @pl.loop(0, nx // BLOCK)
        def _(b):
            add_halo(
                lambda k, part: near[step, k + core * (PAD - 1 - 2 * k), part],
                lambda k: plane(depth - 1 - k),
                target, pad, pl.ds(pl.multiple_of(b * BLOCK, BLOCK), BLOCK),
            )

    def add_far(step, i, target, pad):
        far_copy(step, i).wait_recv()
        add_halo(
            lambda k, part: far[step, (PAD - 1 - k) + core * (2 * k - PAD + 1), part],
            plane, target, pad, rows_of(i),
        )

    add_near(0, older, PAD)
    near_copy(1).start()

    @pl.loop(1, quads)
    def _(g):
        mix(1, older, quad(g))
        pass_on(0, 2 * g - 2, 2)

    @pl.loop(2, quads)
    def _(g):
        update(quad(g), older, newer, PAD, field.at[0], 0)

    @pl.when(has_far)
    def _():
        @pl.loop(0, CHUNKS)
        def _(i):
            add_far(0, order(i), older, PAD)
            send_far(1, i)

    mix(1, older, quad(0))

    @pl.loop(0, 2)
    def _(g):
        update(quad(g), older, newer, PAD, field.at[0], 0)

    add_near(1, field.at[0], 0)

    half = rows // 2
    even = jnp.where(iota((ny // 2, ny), 1) == 2 * iota((ny // 2, ny), 0), 1.0, 0.0).astype(jnp.bfloat16)

    def terms_of(planes):
        size = planes[0].shape[0]
        value = jnp.concatenate(planes, axis=0)
        pieces = []
        for _ in range(3):
            pieces.append(value.astype(jnp.bfloat16))
            value = value - pieces[-1].astype(jnp.float32)
        columns = dot_nt(jnp.concatenate(pieces, axis=0), even).astype(jnp.bfloat16)
        count = 3 * len(planes)
        columns = jnp.concatenate([columns[n * size : (n + 1) * size] for n in range(count)], axis=1)
        picked = dot(even[: size // 2, :size], columns)
        width = ny // 2
        result = []
        for k in range(len(planes)):
            one, two, three = (picked[:, (k + p * len(planes)) * width :][:, :width] for p in range(3))
            sample = one + two + three
            result.append(jnp.log(1.0 + sample * sample))
        return result

    count = PAD // 2
    first_early, first_late = (1 - core) * count, core * (depth // 2 - count)

    @pl.loop(0, depth // 2 - count, step=2)
    def _(q):
        for k, term in enumerate(terms_of([field[0, 2 * (first_early + q + k)] for k in range(2)])):
            early[:, q + k] = term.reshape(CHUNKS, half, ny // 2)

    def to_x(hop, which):
        other = lax.rem(my_x + hop, 4)
        return pltpu.make_async_remote_copy(
            early.at[other * 2 + which], from_x.at[which, hop - 1], x_send.at[which, hop - 1], x_recv.at[which, hop - 1],
            device_id={"group": other * 2 + my_z},
        )

    away, mine = my_x * 2 + 1 - my_z, group
    to_z = pltpu.make_async_remote_copy(early.at[away], from_z, z_send, z_recv, device_id={"group": away})

    @pl.loop(0, 6)
    def _(n):
        to_x(1 + lax.rem(n, 3), lax.rem(1 - my_z + n // 3, 2)).start()

    def sum_x(which):
        total = early[my_x * 2 + which]
        for hop in range(1, 4):
            to_x(hop, which).wait_recv()
            total += from_x[which, hop - 1]
        return total

    def late_terms(i):
        @pl.when(has_far)
        def _():
            add_far(1, i, field.at[0], 0)

        part = rows_of(i)
        return terms_of([field[0, 2 * (first_late + q), part] for q in range(count)])

    def to_owner(i):
        return pltpu.make_async_remote_copy(
            late.at[i], from_late.at[i], late_send.at[i], late_recv.at[i],
            device_id={"group": lax.rem(my_x + 1 + i, 4) * 2 + my_z},
        )

    def late_chunk(i):
        for q, term in enumerate(late_terms(i)):
            late[i, q] = term

        @pl.when(i != 3)
        def _():
            to_owner(i).start()

        @pl.when(jnp.logical_not(has_far))
        def _():
            pass_on(1, i, 1)

    @pl.when(has_far)
    def _():
        pass_on(1, 0, 2 * ROWS - 2)

    @pl.loop(0, 2)
    def _(i):
        late_chunk(i)

    @pl.loop(2, 5)
    def _(i):
        late_chunk(i)

    late_to_z = pltpu.make_async_remote_copy(
        away_late, from_late_z, late_z_send, late_z_recv, device_id={"group": away}
    )
    early[away] = sum_x(1 - my_z)
    to_z.start()
    early[mine] = sum_x(my_z)

    for i in range(3):
        to_owner(i).wait_recv()
    away_late[...] = late[3] + (from_late[0] + from_late[1] + from_late[2])
    late_to_z.start()

    @pl.loop(5, CHUNKS - 1)
    def _(i):
        late_chunk(i)

    to_z.wait_recv()
    at_early = pl.ds(first_early, depth // 2 - count)
    image_out[at_early] = image_ref[at_early] + (jnp.exp((early[mine] + from_z[...]) * 0.125) - 1.0)
    last = late_terms(CHUNKS - 1)
    for i in range(4, CHUNKS - 1):
        to_owner(i).wait_recv()
    late_to_z.wait_recv()
    for q in range(count):
        total = last[q] + (from_late[4, q] + from_late[5, q]) + (from_late[6, q] + from_late_z[q])
        image_out[first_late + q] = image_ref[first_late + q] + (jnp.exp(total * 0.125) - 1.0)

    late_to_z.wait_send()
    to_z.wait_send()
    for step in range(2):
        near_copy(step).wait_send()

    @pl.loop(0, 6)
    def _(n):
        to_x(1 + n // 2, lax.rem(n, 2)).wait_send()

    @pl.loop(0, CHUNKS - 1)
    def _(i):
        @pl.when(i != 3)
        def _():
            to_owner(i).wait_send()

    for step in range(2):
        @pl.loop(0, relayed)
        def _(i):
            pass_copy(step, partner_order(i)).wait_send()

    @pl.when(has_far)
    def _():
        @pl.loop(0, CHUNKS)
        def _(i):
            for step in range(2):
                far_copy(step, i).wait_send()


def write_out(field, image, field_hbm, image_hbm, sems):
    parts = sems.shape[0] - 1
    planes = field.shape[1] // parts
    copies = [
        pltpu.make_async_copy(field.at[:, pl.ds(i * planes, planes)], field_hbm.at[:, pl.ds(i * planes, planes)], sems.at[i])
        for i in range(parts)
    ]
    copies.append(pltpu.make_async_copy(image, image_hbm, sems.at[parts]))
    for copy in copies:
        copy.start()
    for copy in copies:
        copy.wait()


def on_device(prev_field, curr_field, coefficient, recordings, receivers, image_in):
    depth, nx, ny = coefficient.shape
    _, steps, count = recordings.shape
    padded = (depth + 2 * PAD, nx, ny)
    image = image_in.shape
    early, late = (image[0] - PAD // 2,) + image[1:], (PAD // 2,) + image[1:]
    anywhere = pl.BlockSpec(memory_space=pl.ANY)
    vmem = pl.BlockSpec(memory_space=pltpu.VMEM)
    dma = pltpu.SemaphoreType.DMA
    f32 = jnp.float32
    field, image_out = pl.pallas_call(
        kernel,
        out_shape=(pltpu.VMEM(curr_field.shape, f32), pltpu.VMEM(image, f32)),
        in_specs=[anywhere, anywhere, anywhere, vmem, vmem, vmem],
        out_specs=(vmem, vmem),
        scratch_shapes=[
            pltpu.VMEM(padded, f32),
            pltpu.VMEM(padded, f32),
            pltpu.VMEM((depth, nx, ny), f32),
            pltpu.VMEM((steps, PAD, nx, ny), f32),
            pltpu.VMEM((steps, PAD, nx, ny), f32),
            pltpu.VMEM((steps, PAD, nx, ny), f32),
            pltpu.VMEM((depth, nx, ny), f32),
            pltpu.VMEM((nx, nx), jnp.bfloat16),
            pltpu.VMEM((steps, 2, ny, count), jnp.bfloat16),
            pltpu.VMEM((CHUNKS,) + early, f32),
            pltpu.VMEM((CHUNKS - 1,) + late, f32),
            pltpu.VMEM((2, 3) + early, f32),
            pltpu.VMEM(early, f32),
            pltpu.VMEM((CHUNKS - 1,) + late, f32),
            pltpu.VMEM(late, f32),
            pltpu.VMEM(late, f32),
            dma((3,)), dma((steps, CHUNKS)), dma((steps, CHUNKS)), dma((steps,)), dma((steps,)),
            dma((steps, CHUNKS)), dma((steps, CHUNKS)),
            dma((2, 3)), dma((2, 3)), dma, dma, dma((CHUNKS - 1,)), dma((CHUNKS - 1,)), dma, dma,
        ],
        compiler_params=pltpu.CompilerParams(
            collective_id=0, has_side_effects=True, vmem_limit_bytes=59 * 1024 * 1024
        ),
    )(prev_field, curr_field, coefficient, recordings, receivers, image_in)
    return pl.pallas_call(
        write_out,
        out_shape=(jax.ShapeDtypeStruct(curr_field.shape, f32), jax.ShapeDtypeStruct(image, f32)),
        in_specs=[vmem, vmem],
        out_specs=(anywhere, anywhere),
        scratch_shapes=[dma((9,))],
        compiler_params=pltpu.CompilerParams(vmem_limit_bytes=1024 * 1024),
    )(pltpu.with_memory_space_constraint(field, pltpu.VMEM), pltpu.with_memory_space_constraint(image_out, pltpu.VMEM))


def solution(mesh):
    placed = (
        P("group", "space", None, None),
        P("group", "space", None, None),
        P("space", None, None),
        P("group", None, None),
        P("group", None),
        P("space", "group", None),
    )
    return jax.shard_map(
        on_device,
        mesh=mesh,
        in_specs=placed,
        out_specs=(P("group", "space", None, None), P("space", "group", None)),
        check_vma=False,
    )
```
